512 devices in a mesh: occ: 8 (over x, z_hi), vw: 32 (over y, z_lo), vn: 2 (over core).
Axes of the slice: x: 4, y: 8, z: 8 (z_hi: 2, z_lo: 4; z = z_hi * 4 + z_lo), core: 2. Of those that a mesh axis runs over, the one named last changes fastest.
Arguments:
- slabs: bfloat16 [8, 5120, 10240], P('occ', 'vw', 'vn'), may hold values from -0.125 to 0.125
- pair_list: int32 [1, 2], replicated, may hold values from 0 to 7
- occ_energy: float32 [8], replicated, may hold values from -1.2 to -0.4
- virt_energy: float32 [5120], replicated, may hold values from 0.2 to 2.5
Outputs:
- density: float32 [5120, 5120], P('vw', ('occ', 'vn'))
The draws below stay inside these ranges and needn't reach their ends.
Inputs may be any that keep to these rules, and one draw needn't show every extreme that they name: `pair_list`: entries are orbital indices of the window; both entries of a pair may be equal.
All inputs are finite; a program needn't handle non-finite values.
Results may differ from the reference program's by a relative error of at most 0.0035.
Values may be sent and summed in bfloat16 or wider, within the bound.
A program may use at most 64 MiB of HBM per device.

```python
import jax
import jax.numpy as jnp
from jax import lax

V = 5120
Q = 10240
NPAIRS = 1
NOCC = 8


def steps_of(rng, extent, shards, smallest, high):
    def one(position, parts):
        heights = jax.random.uniform(jax.random.fold_in(jax.random.fold_in(rng, 6), position), (parts,), jnp.float32, smallest / len(shards), high / len(shards))
        return jnp.repeat(jnp.exp(heights), extent[position] // parts).reshape((-1,) + (1,) * (len(extent) - position - 1))

    loudness = one(*shards[0])
    for cut in shards[1:]:
        loudness = loudness * one(*cut)
    return loudness


def bell_draw(rng, extent, spread, reach, split=(), dtype=jnp.bfloat16):
    gain = steps_of(rng, extent, split, -0.22, 0.18) if split else 1.0
    result = jax.random.normal(rng, extent, jnp.float32) * spread * gain
    return jnp.minimum(jnp.maximum(result, -reach), reach).astype(dtype)


def setup_inputs(seed: int = 0) -> dict:
    key_of = jax.random.split(jax.random.key(seed), 5)
    slabs = bell_draw(key_of[0], (NOCC, V, Q), (1.8 * (Q * V) ** -0.25), 0.125, ((0, 8), (1, 32), (2, 2)))
    pair_list = jax.random.randint(key_of[1], (NPAIRS, 2), 0, NOCC).astype(jnp.int32)
    occ_energy = jnp.clip(jax.random.uniform(key_of[2], (NOCC,), jnp.float32, -1.2, -0.4), -1.2, -0.4)
    virt_energy = jnp.clip(jax.random.uniform(key_of[3], (V,), jnp.float32, 0.2, 2.5), 0.2, 2.5)
    return {"slabs": slabs, "pair_list": pair_list, "occ_energy": occ_energy, "virt_energy": virt_energy}


def reference(slabs, pair_list, occ_energy, virt_energy):
    density = jnp.zeros((V, V), jnp.float32)
    for index in range(NPAIRS):
        first = pair_list[index, 0]
        second = pair_list[index, 1]
        row_slab = lax.dynamic_index_in_dim(slabs, first, 0, keepdims=False)
        col_slab = lax.dynamic_index_in_dim(slabs, second, 0, keepdims=False)
        integrals = jnp.dot(row_slab, col_slab.T, preferred_element_type=jnp.float32)
        denom = occ_energy[first] + occ_energy[second] - virt_energy[:, None] - virt_energy[None, :]
        amplitudes = (integrals / denom).astype(jnp.bfloat16)
        density = density + jnp.dot(amplitudes, amplitudes.T, preferred_element_type=jnp.float32)
    return density
```

```python
import jax
import jax.numpy as jnp
from jax import lax
from jax.experimental import pallas as pl
from jax.experimental.pallas import tpu as pltpu
from jax.sharding import PartitionSpec as P

NX, NY, NZH, NZL = 4, 8, 2, 4
NZ = NZH * NZL
CHUNKS = 5
EARLY = 3
T_CHUNKS = 5
D_CHUNKS = 5
WINDOW = 2
MESH = pl.DeviceIdType.MESH


def place():
    occ = lax.axis_index("occ")
    vw = lax.axis_index("vw")
    v = lax.axis_index("vn")
    return occ // NZH, vw // NZL, (occ % NZH) * NZL + vw % NZL, v


def device(x, y, z, v):
    return {"occ": x * NZH + z // NZL, "vw": y * NZL + z % NZL, "vn": v}


def greet(partners):
    barrier = pltpu.get_barrier_semaphore()
    for partner in partners:
        pl.semaphore_signal(barrier, inc=1, device_id=partner, device_id_type=MESH)
    pl.semaphore_wait(barrier, len(partners))


def remote(src, dst, send_sem, recv_sem, target):
    return pltpu.make_async_remote_copy(
        src_ref=src,
        dst_ref=dst,
        send_sem=send_sem,
        recv_sem=recv_sem,
        device_id=target,
        device_id_type=MESH,
    )


def natural(z):
    return (z % NZL) * NZH + z // NZL


def dot(left, right):
    return lax.dot_general(
        left, right, (((1,), (1,)), ((), ())), preferred_element_type=jnp.float32
    )


class Ring:
    def __init__(self, out, index, count, chunks, window, slot, target, sems):
        self.out, self.index, self.count, self.chunks = out, index, count, chunks
        self.window, self.slot, self.target = window, slot, target
        self.send_sem, self.recv_sem = sems
        self.last = count // 2
        self.copies = {}

    def ways(self, step, chunk):
        return (0, 1) if step < self.last else (chunk % 2,)

    def origin(self, way, step):
        sign = 1 if way == 0 else -1
        return (self.index - sign * step + self.count) % self.count

    def start(self, way, step, chunk):
        sign = 1 if way == 0 else -1
        ref = self.window(self.slot(self.origin(way, step - 1)), chunk)
        k = (way * self.last + step - 1) * self.chunks + chunk
        copy = remote(
            ref,
            ref,
            self.send_sem.at[k],
            self.recv_sem.at[k],
            self.target((self.index + sign + self.count) % self.count),
        )
        self.copies[(way, step, chunk)] = copy
        copy.start()

    def begin(self, chunk):
        for way in self.ways(1, chunk):
            self.start(way, 1, chunk)

    def advance(self, step, chunk):
        for way in self.ways(step, chunk):
            self.copies[(way, step, chunk)].wait_recv()
            if step < self.last and way in self.ways(step + 1, chunk):
                self.start(way, step + 1, chunk)

    def finish(self):
        for copy in self.copies.values():
            copy.wait_send()


def ring_sems(count, chunks):
    return [pltpu.SemaphoreType.DMA((count * chunks,))] * 2


def kernel(
    pair_in, occ_in, slab, row_in, col_in, out,
    pair, occ_energy, row_energy, col_energy, small_sem,
    fetched, chosen, swapped, block_a, block_c, part, inbox, mine, parts,
    all_rows, column, columns, terms, running, landed,
    fetch_send, fetch_recv, fetch_local, swap_send, swap_recv,
    c_send, c_recv, a_send, a_recv, core_send, core_recv, sum_send, sum_recv,
    t_send, t_recv, along_send, along_recv, across_send, across_recv,
    b_send, b_recv, b_local, d_send, d_recv,
):
    x, y, z, v = place()
    zh = z // NZL
    half = swapped.shape[2]
    width = fetched.shape[3]
    depth = width * CHUNKS
    bf16, f32 = jnp.bfloat16, jnp.float32
    other = device(x, y, z, 1 - v)
    x_peers = [device((x + d) % NX, y, z, v) for d in range(1, NX)]
    z_peers = [device(x, y, (z + d) % NZ, v) for d in range(1, NZ)]
    y_peers = [device(x, (y + d) % NY, z, v) for d in (1, NY - 1)]
    small = [
        pltpu.make_async_copy(source, target, small_sem.at[n])
        for n, (source, target) in enumerate(
            [(pair_in, pair), (occ_in, occ_energy), (row_in, row_energy), (col_in, col_energy)]
        )
    ]
    for copy in small:
        copy.start()
    greet([other] + x_peers + y_peers + [z_peers[0], z_peers[NZL - 1], z_peers[NZ - 2]])

    fetches = {}

    def fetch(c):
        for d in (2, 1, 3, 0):
            target = (x + d) % NX
            cols = pl.ds(pl.multiple_of(target * depth + c * width, 128), width)
            if d:
                copy = remote(
                    slab.at[:, cols],
                    fetched.at[c, x],
                    fetch_send.at[c * NX + d],
                    fetch_recv.at[c * NX + d],
                    x_peers[d - 1],
                )
            else:
                copy = pltpu.make_async_copy(
                    slab.at[:, cols], fetched.at[c, x], fetch_local.at[c]
                )
            copy.start()
            fetches[(c, d)] = copy

    for c in range(min(WINDOW, CHUNKS)):
        fetch(c)

    for copy in small:
        copy.wait()
    orbitals = (pair[0, 0], pair[0, 1])
    ring_c = Ring(
        block_c, y, NY, CHUNKS,
        lambda s, c: block_c.at[s, :, pl.ds(c * width, width)],
        lambda k: k, lambda k: device(x, k, z, v), (c_send, c_recv),
    )
    early = pl.ds(0, EARLY * width)
    late = pl.ds(EARLY * width, (CHUNKS - EARLY) * width)
    ring_a = Ring(
        block_a, z, NZ, 2,
        lambda s, c: block_a.at[s, :, early if c == 0 else late],
        natural, lambda k: device(x, y, k, v), (a_send, a_recv),
    )
    def drain():
        for c in range(max(CHUNKS - WINDOW, 0), CHUNKS):
            for d in range(1, NX):
                fetches[(c, d)].wait_send()
        for copy in swaps.values():
            copy.wait_send()
        ring_c.finish()
        ring_a.finish()
        for n in range(NZ):
            @pl.when(owner(order[n])[0] != v)
            def _():
                core_copy(n).wait_send()
        for d in range(1, NX):
            sum_copy(0, d).wait_send()
        ring_t.finish()
        for copy in list(along.values()) + across:
            copy.wait_send()
        for parity in range(NZH):
            for d in range(1, NX):
                for chunk in range(T_CHUNKS):
                    b_copy(0, parity, d, x, chunk).wait_send()
        for chunk in range(D_CHUNKS):
            for way in range(2):
                for step in range(chain(way, chunk)):
                    d_copy(way, step, chunk).wait_send()

    swaps = {}

    def select(c):
        for d in range(NX):
            if d:
                fetches[(c, d)].wait_recv()
            else:
                fetches[(c, d)].wait()
        if c + WINDOW < CHUNKS:
            for d in range(1, NX):
                fetches[(c, d)].wait_send()
            fetch(c + WINDOW)
        for k in (1, 0):
            source = orbitals[k] // NZH
            value = fetched[c, 0]
            for n in range(1, NX):
                value = jnp.where(source == n, fetched[c, n], value)
            chosen[c, k] = value
            first = pl.multiple_of((1 - zh) * half, 16)
            swaps[(c, k)] = remote(
                chosen.at[c, k, pl.ds(first, half)],
                swapped.at[c, k],
                swap_send.at[c * 2 + k],
                swap_recv.at[c * 2 + k],
                z_peers[NZL - 1],
            )
            swaps[(c, k)].start()

    def settle(c, k):
        swaps[(c, k)].wait_recv()
        kept = chosen[c, k, pl.ds(pl.multiple_of(zh * half, 16), half), :]
        value = jnp.where(orbitals[k] % NZH == zh, kept, swapped[c, k])
        cols = pl.ds(c * width, width)
        if k:
            block_c[y, :, cols] = value
        else:
            block_a[natural(z), :, cols] = value

    def advance_c(tick):
        for c in range(CHUNKS):
            step = tick - 1 - c
            if 1 <= step <= ring_c.last:
                ring_c.advance(step, c)

    for tick in range(CHUNKS + 1):
        if tick < CHUNKS:
            select(tick)
        advance_c(tick)
        if tick == CHUNKS:
            ring_a.advance(1, 0)
        if tick:
            settle(tick - 1, 1)
            ring_c.begin(tick - 1)
            settle(tick - 1, 0)
            if tick == EARLY:
                ring_a.begin(0)
    ring_a.begin(1)
    advance_c(CHUNKS + 1)
    ring_a.advance(2, 0)
    ring_a.advance(1, 1)
    advance_c(CHUNKS + 2)
    ring_a.advance(3, 0)
    ring_a.advance(2, 1)
    advance_c(CHUNKS + 3)
    advance_c(CHUNKS + 4)
    rows = part.shape[1]

    def owner(position):
        k = natural(position)
        return k // NX, k % NX

    def core_copy(n):
        return remote(
            part.at[n], inbox.at[n], core_send.at[n], core_recv.at[n], other
        )

    def integrals(n, position):
        part[n] = dot(
            block_a[natural(position)],
            block_c[...].reshape(NY * half, depth),
        )

        @pl.when(owner(position)[0] != v)
        def _():
            core_copy(n).start()

    def sum_copy(n, d):
        return remote(
            part.at[n],
            parts.at[d - 1],
            sum_send.at[d - 1],
            sum_recv.at[d - 1],
            x_peers[d - 1],
        )

    def combine(n, position):
        vk, xk = owner(position)

        @pl.when(vk == v)
        def _():
            core_copy(n).wait_recv()

            @pl.when(xk == x)
            def _():
                mine[...] = part[n] + inbox[n]

            @pl.when(xk != x)
            def _():
                part[n] = part[n] + inbox[n]

            for d in range(1, NX):
                @pl.when(xk == (x + d) % NX)
                def _():
                    sum_copy(n, d).start()

    order = [z] + [(z + s + NZ) % NZ for s in (-1, 1, -2, 2, -3, 3, 4)]
    def blocks(first, last):
        for n in range(first, last):
            integrals(n, order[n])
            if n:
                combine(n - 1, order[n - 1])

    blocks(0, 2)
    ring_a.advance(3, 1)
    blocks(2, 5)
    ring_a.advance(4, 0)
    ring_a.advance(4, 1)
    blocks(5, 8)
    combine(7, order[7])

    for d in range(1, NX):
        sum_copy(0, d).wait_recv()
    total = (mine[...] + parts[0]) + (parts[1] + parts[2])
    pair_energy = occ_energy[orbitals[0]] + occ_energy[orbitals[1]]
    denom = pair_energy - row_energy[...] - col_energy[...]
    amplitude = (total / denom).astype(bf16)
    slot = v * NX + x
    all_rows[slot] = amplitude
    column[y] = amplitude

    t_rows = rows // T_CHUNKS
    ring_t = Ring(
        column, y, NY, T_CHUNKS,
        lambda s, c: column.at[s, pl.ds(c * t_rows, t_rows)],
        lambda k: k, lambda k: device(x, k, z, v), (t_send, t_recv),
    )

    def b_copy(group, parity, d, source, chunk):
        window = pl.ds(chunk * t_rows, t_rows)
        k = (parity * NX + d) * T_CHUNKS + chunk
        return remote(
            column.at[group, window],
            columns.at[parity, source, window],
            b_send.at[k],
            b_recv.at[k],
            x_peers[d - 1],
        )

    def b_keep(group, parity):
        return pltpu.make_async_copy(
            column.at[group], columns.at[parity, x], b_local.at[parity]
        )

    def deliver(group, chunk):
        goal, parity = group // NZH, group % NZH

        @pl.when(goal != x)
        def _():
            window = pl.ds(chunk * t_rows, t_rows)
            k = (parity * NX + (goal - x + NX) % NX) * T_CHUNKS + chunk
            remote(
                column.at[group, window],
                columns.at[parity, x, window],
                b_send.at[k],
                b_recv.at[k],
                device(goal, y, z, v),
            ).start()

        if chunk == T_CHUNKS - 1:
            @pl.when(x == goal)
            def _():
                b_keep(group, parity).start()

    for chunk in range(T_CHUNKS):
        ring_t.begin(chunk)
    across = [
        remote(
            all_rows.at[slot], all_rows.at[slot], across_send.at[0], across_recv.at[0], other
        )
    ]
    across[0].start()
    along = {}
    for d in (2, 1, 3):
        along[d] = remote(
            all_rows.at[slot],
            all_rows.at[slot],
            along_send.at[d],
            along_recv.at[d],
            x_peers[d - 1],
        )
        along[d].start()
    for chunk in range(T_CHUNKS):
        deliver(y, chunk)

    def pass_on(d):
        along[d].wait_recv()
        source = v * NX + (x - d + NX) % NX
        copy = remote(
            all_rows.at[source],
            all_rows.at[source],
            across_send.at[d],
            across_recv.at[d],
            other,
        )
        copy.start()
        across.append(copy)

    for step in range(1, ring_t.last + 1):
        for chunk in range(T_CHUNKS):
            ring_t.advance(step, chunk)
            deliver(ring_t.origin(0, step), chunk)
            if step < ring_t.last:
                deliver(ring_t.origin(1, step), chunk)
        if step == 2:
            for d in (1, 3, 2):
                pass_on(d)
    for copy in across:
        copy.wait_recv()
    for parity in range(NZH):
        for d in range(1, NX):
            for chunk in range(T_CHUNKS):
                b_copy(0, parity, d, (x - d + NX) % NX, chunk).wait_recv()
        b_keep(0, parity).wait()

    tile = 2 * half

    d_rows = tile // D_CHUNKS

    def terms_of(position):
        left = all_rows[pl.ds((position % NZL) * 2, 2)].reshape(tile, NY * half)
        right = columns[position // NZL].reshape(NX * rows, NY * half)
        return dot(left, right)

    def chain(way, chunk):
        return NZ // 2 if way == chunk % 2 else NZ // 2 - 1

    def d_copy(way, step, chunk):
        k = (way * (NZ // 2) + step) * D_CHUNKS + chunk
        return remote(
            running.at[k],
            landed.at[k],
            d_send.at[k],
            d_recv.at[k],
            z_peers[0] if way == 0 else z_peers[NZ - 2],
        )

    def toward(way, distance):
        return (z + (1 - 2 * way) * distance + NZ) % NZ

    def emit(way, step, chunk):
        window = pl.ds(chunk * d_rows, d_rows)
        distance = chain(way, chunk) - step
        value = terms[distance * 2 + way if distance < NZ // 2 else NZ, window]
        k = (way * (NZ // 2) + step) * D_CHUNKS + chunk
        if step:
            d_copy(way, step - 1, chunk).wait_recv()
            value = value + landed[k - D_CHUNKS].astype(f32)
        running[k] = value.astype(bf16)
        d_copy(way, step, chunk).start()

    last = NZ // 2
    terms[NZ] = terms_of(toward(0, last))
    for chunk in range(D_CHUNKS):
        emit(chunk % 2, 0, chunk)
    for way in range(2):
        terms[(last - 1) * 2 + way] = terms_of(toward(way, last - 1))
        for chunk in range(D_CHUNKS):
            if chunk % 2 != way:
                emit(way, 0, chunk)
    for step in range(1, last):
        if step < last - 1:
            for way in range(2):
                terms[(last - 1 - step) * 2 + way] = terms_of(toward(way, last - 1 - step))
        else:
            terms[0] = terms_of(z)
        for chunk in range(D_CHUNKS):
            for way in range(2):
                if step < chain(way, chunk):
                    emit(way, step, chunk)
    for chunk in range(D_CHUNKS):
        window = pl.ds(chunk * d_rows, d_rows)
        value = terms[0, window]
        for way in range(2):
            step = chain(way, chunk) - 1
            d_copy(way, step, chunk).wait_recv()
            value = value + landed[(way * last + step) * D_CHUNKS + chunk].astype(f32)
        out[window] = value
    drain()


def per_device(slabs, pair_list, occ_energy, virt_energy):
    x, y, z, v = place()
    tile, depth = slabs.shape[1], slabs.shape[2]
    half = tile // NZH
    q = depth // NX
    group = NZL * tile
    width = NY * half
    rows = group // (2 * NX)
    bf16, f32 = jnp.bfloat16, jnp.float32
    row_energy = lax.dynamic_slice_in_dim(
        virt_energy, y * group + (v * NX + x) * rows, rows
    ).reshape(rows, 1)
    col_energy = lax.dynamic_slice(
        virt_energy.reshape(NY, NZL, NZH, half),
        (0, z % NZL, z // NZL, 0),
        (NY, 1, 1, half),
    ).reshape(1, width)
    vmem = pl.BlockSpec(memory_space=pltpu.VMEM)

    def sems(n):
        return [pltpu.SemaphoreType.DMA((n,))] * 2

    return pl.pallas_call(
        kernel,
        out_shape=jax.ShapeDtypeStruct((tile, NX * rows), f32),
        in_specs=[pl.BlockSpec(memory_space=pltpu.HBM)] * 3
        + [pl.BlockSpec(memory_space=pl.ANY)] * 2,
        out_specs=vmem,
        scratch_shapes=[
            pltpu.SMEM((1, 2), jnp.int32),
            pltpu.SMEM((NX * NZH,), f32),
            pltpu.VMEM((rows, 1), f32),
            pltpu.VMEM((1, width), f32),
            pltpu.SemaphoreType.DMA((4,)),
            pltpu.VMEM((CHUNKS, NX, tile, q // CHUNKS), bf16),
            pltpu.VMEM((CHUNKS, 2, tile, q // CHUNKS), bf16),
            pltpu.VMEM((CHUNKS, 2, half, q // CHUNKS), bf16),
            pltpu.VMEM((NZ, half, q), bf16),
            pltpu.VMEM((NY, half, q), bf16),
            pltpu.VMEM((NZ, rows, width), f32),
            pltpu.VMEM((NZ, rows, width), f32),
            pltpu.VMEM((rows, width), f32),
            pltpu.VMEM((NX - 1, rows, width), f32),
            pltpu.VMEM((2 * NX, rows, width), bf16),
            pltpu.VMEM((NY, rows, width), bf16),
            pltpu.VMEM((NZH, NX, rows, width), bf16),
            pltpu.VMEM((NZ + 1, tile, NX * rows), f32),
            pltpu.VMEM((NZ * D_CHUNKS, tile // D_CHUNKS, NX * rows), bf16),
            pltpu.VMEM((NZ * D_CHUNKS, tile // D_CHUNKS, NX * rows), bf16),
        ]
        + sems(CHUNKS * NX)
        + [pltpu.SemaphoreType.DMA((CHUNKS,))]
        + sems(CHUNKS * 2)
        + ring_sems(NY, CHUNKS)
        + ring_sems(NZ, 2)
        + sems(NZ)
        + sems(NX - 1)
        + ring_sems(NY, T_CHUNKS)
        + sems(NX)
        + sems(NX)
        + sems(NZH * NX * T_CHUNKS)
        + [pltpu.SemaphoreType.DMA((NZH,))]
        + sems(NZ * D_CHUNKS),
        compiler_params=pltpu.CompilerParams(
            collective_id=0, has_side_effects=True, vmem_limit_bytes=66 * 10**6
        ),
    )(pair_list, occ_energy, slabs.reshape(tile, depth), row_energy, col_energy)


def solution(mesh):
    return jax.shard_map(
        per_device,
        mesh=mesh,
        in_specs=(P("occ", "vw", "vn"), P(), P(), P()),
        out_specs=P("vw", ("occ", "vn")),
        check_vma=False,
    )
```
